32 devices in a mesh: seq: 8 (over z, y), res: 4 (over x, core).
Axes of the slice: x: 2, y: 2, z: 4, core: 2. Of those that a mesh axis runs over, the one named last changes fastest.
Arguments:
- target_alignment_matrix: float32 [512, 32, 256], P('seq', 'res'), may hold values from -6 to 6
- source_alignment_matrix: float32 [512, 128, 256], P('seq', 'res'), may hold values from -6 to 6
- source_mapping_matrix: float32 [256, 32], replicated, may hold values from -0.375 to 0.375
- target_mapping_matrix: float32 [256, 32], replicated, may hold values from -0.375 to 0.375
- final_mapping_matrix: float32 [1024, 128], replicated, may hold values from -4.2426405 to 4.2426405
- edge_offset_vector: float32 [128], replicated, may hold values from -3 to 3
- edge_delta_cotangent: float32 [128, 32, 128], P('seq', 'res'), may hold values from -6 to 6
Outputs:
- edge_delta_result: float32 [128, 32, 128], P('seq', 'res')
- grad_cols: float32 [512, 32, 256], P('seq', 'res')
- grad_rows: float32 [512, 128, 256], P('seq', 'res')
- grad_left: float32 [256, 32], replicated
- grad_right: float32 [256, 32], replicated
- grad_proj: float32 [1024, 128], replicated
- grad_bias: float32 [128], replicated
The draws below stay inside these ranges and needn't reach their ends.
All inputs are finite; a program needn't handle non-finite values.
Results may differ from the reference program's by a relative error of at most 0.00013.
Values sent between devices are 32-bit elements; how exact they have to be, the bound alone decides.
No kernel may reach another device: no remote copies, remote signals or barrier semaphores. Data moves between devices by JAX's collectives and lax.ppermute only.
A program may use at most 64 MiB of HBM per device.

```python
import jax
import jax.numpy as jnp
from jax import lax

ALIGN_FEATURES = 256
HIDDEN_WIDTH = 32
EDGE_FEATURES = 128
SOURCE_AMINOS = 128
ALIGN_MEMBERS = 512
TARGET_AMINOS = 32


def levels(rng, shape, cuts, low, high):
    def one(axis_at, parts):
        draws = jax.random.uniform(jax.random.fold_in(jax.random.fold_in(rng, 6), axis_at), (parts,), jnp.float32, low / len(cuts), high / len(cuts))
        return jnp.repeat(jnp.exp(draws), shape[axis_at] // parts).reshape((-1,) + (1,) * (len(shape) - axis_at - 1))

    factor_of = one(*cuts[0])
    for cut in cuts[1:]:
        factor_of = factor_of * one(*cut)
    return factor_of


def scatter_about(stream_key, dims, scale, bound, cuts=(), kind=jnp.bfloat16):
    values = jax.random.normal(stream_key, dims, jnp.float32) * scale
    if len(cuts) > 0:
        values = levels(stream_key, dims, cuts, -0.22, 0.18) * values
    return jnp.clip(values, min=-bound, max=bound).astype(kind)


def setup_inputs(seed: int = 0) -> dict:
    streams_of = jax.random.split(jax.random.key(seed), 8)
    return {
        "target_alignment_matrix": scatter_about(streams_of[0], (ALIGN_MEMBERS, TARGET_AMINOS, ALIGN_FEATURES), 1.0, 6.0, ((0, 8), (1, 4)), jnp.float32),
        "source_alignment_matrix": scatter_about(streams_of[1], (ALIGN_MEMBERS, SOURCE_AMINOS, ALIGN_FEATURES), 1.0, 6.0, ((0, 8), (1, 4)), jnp.float32),
        "source_mapping_matrix": scatter_about(streams_of[2], (ALIGN_FEATURES, HIDDEN_WIDTH), ALIGN_FEATURES ** -0.5, 0.375, (), jnp.float32),
        "target_mapping_matrix": scatter_about(streams_of[3], (ALIGN_FEATURES, HIDDEN_WIDTH), ALIGN_FEATURES ** -0.5, 0.375, (), jnp.float32),
        "final_mapping_matrix": scatter_about(streams_of[4], (HIDDEN_WIDTH * HIDDEN_WIDTH, EDGE_FEATURES), (ALIGN_MEMBERS ** 0.5 * 0.03125), 4.2426405, (), jnp.float32),
        "edge_offset_vector": scatter_about(streams_of[5], (EDGE_FEATURES,), 0.5, 3.0, (), jnp.float32),
        "edge_delta_cotangent": scatter_about(streams_of[6], (SOURCE_AMINOS, TARGET_AMINOS, EDGE_FEATURES), 1.0, 6.0, ((0, 8), (1, 4)), jnp.float32),
    }


def standardize_features(values):
    average = lax.optimization_barrier(jnp.mean(values, axis=-1, keepdims=True))
    centred = values - average
    inverse = lax.rsqrt(lax.optimization_barrier(jnp.mean(centred * centred, axis=-1, keepdims=True)) + 1e-05)
    return centred * inverse

def evaluate_primal(target_alignment_matrix, source_alignment_matrix, source_mapping_matrix, target_mapping_matrix, final_mapping_matrix, edge_offset_vector):
    exact_arithmetic = lax.Precision.HIGHEST
    source_mapped_vectors = jnp.einsum('uwh,hq->uwq', standardize_features(source_alignment_matrix), source_mapping_matrix, precision=exact_arithmetic)
    target_mapped_vectors = jnp.einsum('iwe,ed->iwd', standardize_features(target_alignment_matrix), target_mapping_matrix, precision=exact_arithmetic)
    tensor_average_block = jnp.einsum('ipu,ihl->phul', source_mapped_vectors, target_mapped_vectors, precision=exact_arithmetic) / source_alignment_matrix.shape[0]
    rows_total = source_mapped_vectors.shape[1]
    cols_total = target_mapped_vectors.shape[1]
    square = source_mapped_vectors.shape[2] * target_mapped_vectors.shape[2]
    flat_rows = tensor_average_block.reshape(rows_total * cols_total, square)
    projected = jnp.dot(flat_rows, final_mapping_matrix, precision=exact_arithmetic) + edge_offset_vector
    return projected.reshape(rows_total, cols_total, final_mapping_matrix.shape[1])

def reference(target_alignment_matrix, source_alignment_matrix, source_mapping_matrix, target_mapping_matrix, final_mapping_matrix, edge_offset_vector, edge_delta_cotangent):
    edge_delta_result, adjoint_mapping = jax.vjp(evaluate_primal, target_alignment_matrix, source_alignment_matrix, source_mapping_matrix, target_mapping_matrix, final_mapping_matrix, edge_offset_vector)
    grads = adjoint_mapping(edge_delta_cotangent)
    return (edge_delta_result, grads[0], grads[1], grads[2], grads[3], grads[4], grads[5])
```

```python
import jax
import jax.numpy as jnp
from jax import lax
from jax.sharding import PartitionSpec as P

HIGH = lax.Precision.HIGH


def swap(x, axis, mask):
    n = lax.axis_size(axis)
    return lax.ppermute(x, axis, [(i, i ^ mask) for i in range(n)])


def masks(axis):
    n = lax.axis_size(axis)
    assert n & (n - 1) == 0
    return [1 << b for b in range(n.bit_length() - 1)]


def gather(x, axis):
    me = lax.axis_index(axis)
    for mask in masks(axis):
        other = swap(x, axis, mask)
        up = (me & mask) != 0
        x = jnp.where(up, jnp.concatenate([other, x]), jnp.concatenate([x, other]))
    return x


def scatter_sum(x, axis):
    me = lax.axis_index(axis)
    for mask in masks(axis)[::-1]:
        half = x.shape[0] // 2
        up = ((me & mask) != 0).astype(jnp.int32)
        keep = lax.dynamic_slice_in_dim(x, up * half, half)
        send = lax.dynamic_slice_in_dim(x, (1 - up) * half, half)
        x = keep + swap(send, axis, mask)
    return x


def sum_all(x):
    x = scatter_sum(scatter_sum(x, "res"), "seq")
    return gather(gather(x, "seq"), "res")


def standardize(values):
    average = jnp.mean(values, axis=-1, keepdims=True)
    centred = values - average
    inverse = lax.rsqrt(jnp.mean(centred * centred, axis=-1, keepdims=True) + 1e-05)
    return (centred * inverse, inverse)


def normalize_back(normed, inverse, upstream):
    first = jnp.mean(upstream, axis=-1, keepdims=True)
    second = jnp.mean(upstream * normed, axis=-1, keepdims=True)
    return inverse * (upstream - first - normed * second)


def body(target, source, w_source, w_target, w_final, bias, cot):
    members, cols, _ = target.shape
    hidden = w_source.shape[1]
    square = hidden * hidden
    width = w_final.shape[1]
    total = members * lax.axis_size("seq")
    own_rows = cot.shape[0]
    row_n, row_inv = standardize(source)
    col_n, col_inv = standardize(target)
    left = jnp.einsum("sic,ch->ish", row_n, w_source, precision=HIGH)
    right = jnp.einsum("sjc,ck->sjk", col_n, w_target, precision=HIGH)
    left = gather(left, "res")
    rows = left.shape[0]
    outer = jnp.einsum("ish,sjk->jihk", left, right, precision=HIGH) / total
    outer = outer.reshape(cols * rows, square)
    part = jnp.dot(outer, w_final, precision=HIGH).reshape(cols, rows, width)
    edge = scatter_sum(part.transpose(1, 0, 2), "seq") + bias
    cot_all = gather(cot, "seq").transpose(1, 0, 2).reshape(cols * rows, width)
    grad_proj = jnp.einsum("pa,pb->ab", outer, cot_all, precision=HIGH)
    grad_outer = jnp.dot(cot_all, w_final.T, precision=HIGH).reshape(cols, rows, hidden, hidden)
    grad_ls = jnp.einsum("jihk,sjk->ish", grad_outer, right, precision=HIGH) / total
    grad_rs = jnp.einsum("jihk,ish->sjk", grad_outer, left, precision=HIGH) / total
    grad_ls = scatter_sum(grad_ls, "res")
    g_left = jnp.einsum("sic,ish->hc", row_n, grad_ls, precision=HIGH)
    g_right = jnp.einsum("sjc,sjk->kc", col_n, grad_rs, precision=HIGH)
    g_bias = jnp.sum(cot, axis=(0, 1))
    small = jnp.concatenate([g_left.reshape(-1), g_right.reshape(-1), g_bias])
    unit = width * lax.axis_size("seq") * lax.axis_size("res")
    small = jnp.pad(small, (0, -small.size % unit)).reshape(-1, width)
    both = sum_all(jnp.concatenate([grad_proj, small]))
    grad_proj, small = both[:square], both[square:].reshape(-1)
    n = g_left.size
    g_left = small[:n].reshape(g_left.shape).T
    g_right = small[n : n + g_right.size].reshape(g_right.shape).T
    g_bias = small[n + g_right.size : n + g_right.size + width]
    up_rows = jnp.einsum("ish,ch->sic", grad_ls, w_source, precision=HIGH)
    up_cols = jnp.einsum("sjh,ch->sjc", grad_rs, w_target, precision=HIGH)
    grad_rows = normalize_back(row_n, row_inv, up_rows)
    grad_cols = normalize_back(col_n, col_inv, up_cols)
    return edge, grad_cols, grad_rows, g_left, g_right, grad_proj, g_bias


def solution(mesh):
    split = P("seq", "res", None)
    return jax.shard_map(
        body,
        mesh=mesh,
        in_specs=(split, split, P(), P(), P(), P(), split),
        out_specs=(split, split, split, P(), P(), P(), P()),
        check_vma=False,
    )
```

```python
import functools

import jax
import jax.numpy as jnp
from jax import lax
from jax.experimental import pallas as pl
from jax.experimental.pallas import tpu as pltpu
from jax.sharding import PartitionSpec as P

F32 = jnp.float32
BF16 = jnp.bfloat16
LANES = 128


def swap(x, axis, mask):
    n = lax.axis_size(axis)
    return lax.ppermute(x, axis, [(i, i ^ mask) for i in range(n)])


def masks(axis):
    n = lax.axis_size(axis)
    assert n & (n - 1) == 0
    return [1 << b for b in range(n.bit_length() - 1)]


def xor_ids(order):
    ids = [0]
    for mask in reversed(order):
        ids = ids + [i ^ mask for i in ids]
    return ids


def split(x):
    hi = x.astype(BF16)
    return hi, (x - hi.astype(F32)).astype(BF16)


def dot(a, b, ca, cb):
    return lax.dot_general(a, b, (((ca,), (cb,)), ((), ())), preferred_element_type=F32)


def call(kernel, outs, args, scratch=(), flops=0, name=None):
    nbytes = sum(a.size * 4 for a in args) + sum(4 * functools.reduce(int.__mul__, o) for o in outs)
    return pl.pallas_call(
        kernel,
        name=name,
        out_shape=[jax.ShapeDtypeStruct(o, F32) for o in outs],
        in_specs=[pl.BlockSpec(memory_space=pltpu.VMEM)] * len(args),
        out_specs=[pl.BlockSpec(memory_space=pltpu.VMEM)] * len(outs),
        scratch_shapes=list(scratch),
        compiler_params=pltpu.CompilerParams(vmem_limit_bytes=28 << 20),
        cost_estimate=pl.CostEstimate(flops=flops, bytes_accessed=nbytes, transcendentals=0),
    )(*args)


def low_half(shape):
    return lax.broadcasted_iota(jnp.int32, shape, len(shape) - 1) < LANES // 2


def to_tiles(x_ref, tiles):
    for t in range(2):
        tiles[t] = x_ref[:, t * LANES : (t + 1) * LANES]


def from_tiles(tiles, out_ref):
    for t in range(2):
        out_ref[:, t * LANES : (t + 1) * LANES] = tiles[t]


def norm_group(x_ref, y_ref, inv_ref, i0, group, count, members):
    his, los = [], []
    for g in range(group):
        i = i0 + g
        x = jnp.concatenate([x_ref[t, pl.ds(i, members, stride=count), :] for t in range(2)], 1)
        x = x - jnp.mean(x, axis=-1, keepdims=True)
        inv = lax.rsqrt(jnp.mean(x * x, axis=-1, keepdims=True) + 1e-05)
        y = x * inv
        at = pl.ds(pl.multiple_of(i * members, members), members)
        y_ref[at, :] = y
        inv_ref[at, :] = inv
        hi, lo = split(y)
        his.append(hi)
        los.append(lo)
    return jnp.concatenate(his, 0), jnp.concatenate(los, 0)


def project(w_ref, hi, lo):
    whi, wlo = split(w_ref[...])
    n = whi.shape[0]
    both = dot(jnp.concatenate([whi, wlo], 0), hi, 1, 1)
    return both[:n] + both[n:] + dot(whi, lo, 1, 1)


def rows_kernel(count, members, x_ref, w_ref, left_ref, y_ref, inv_ref, tiles):
    to_tiles(x_ref, tiles)
    hidden = w_ref.shape[0]
    half = hidden // 2
    low = low_half((half, LANES))

    def step(g, carry):
        i0 = g * 4
        hi, lo = norm_group(tiles, y_ref, inv_ref, i0, 4, count, members)
        left = project(w_ref, hi, lo)
        for t in range(2):
            a = left[:half, t * LANES : (t + 1) * LANES]
            b = left[half:, t * LANES : (t + 1) * LANES]
            first = jnp.where(low, a, pltpu.roll(b, LANES // 2, 1))
            second = jnp.where(low, pltpu.roll(a, LANES // 2, 1), b)
            left_ref[pl.ds(i0 + 2 * t, half, stride=count), :] = first
            left_ref[pl.ds(i0 + 2 * t + 1, half, stride=count), :] = second
        return carry

    lax.fori_loop(0, count // 4, step, 0)


def cols_kernel(count, members, scale, x_ref, w_ref, right_ref, y_ref, inv_ref, tiles):
    to_tiles(x_ref, tiles)
    hidden = w_ref.shape[0]
    low = low_half((hidden, LANES))

    for g in range(count // 4):
        hi, lo = norm_group(tiles, y_ref, inv_ref, g * 4, 4, count, members)
        right = project(w_ref, hi, lo) * scale
        for t in range(2):
            v = right[:, t * LANES : (t + 1) * LANES]
            w = pltpu.roll(v, LANES // 2, 1)
            j = g * 4 + 2 * t
            for m, (a, b) in enumerate(((v, w), (w, v))):
                right_ref[pl.ds((j + m) * hidden, hidden), :] = jnp.where(low, a, 0.0)
                right_ref[pl.ds((count + j + m) * hidden, hidden), :] = jnp.where(low, 0.0, b)


def load_left(ids, pieces, full):
    me = lax.axis_index("res")
    for i, piece in zip(ids, pieces):
        n = piece.shape[1]
        full[:, pl.ds(pl.multiple_of((me ^ i) * n, n), n), :] = piece[...]


def load_cot(ids, pieces, full):
    me = lax.axis_index("seq")
    cols = full.shape[0]
    own = pieces[0].shape[0] // cols
    at = 0
    for piece in pieces:
        for b in range(piece.shape[0] // (own * cols)):
            off = pl.multiple_of((me ^ ids[at]) * own, own)
            at += 1
            for j in range(cols):
                full[j, pl.ds(off, own), :] = piece[pl.ds(b * own * cols + j, own, stride=cols), :]


def outer_kernel(left_ids, cot_ids, edge_ids, proj_bits, n_left, n_cot, *refs):
    lefts, refs = refs[:n_left], refs[n_left:]
    cots, refs = refs[:n_cot], refs[n_cot:]
    right_ref, f_ref, edge_keep, edge_send, proj_keep, proj_send = refs[:6]
    left, lhi, llo, ohi, olo, cot, ccat, fcat, edge, proj = refs[6:]
    halves, rows, _ = left.shape
    cols = cot.shape[0]
    width = f_ref.shape[1]
    hidden = 2 * halves
    square = hidden * hidden
    load_left(left_ids, lefts, left)
    load_cot(cot_ids, cots, cot)
    hi, lo = split(left[...].reshape(halves * rows, LANES))
    lhi[...] = hi
    llo[...] = lo
    hi, lo = split(cot[...].reshape(cols * rows, width))
    ccat[:, :width] = hi
    ccat[:, width:] = lo
    for n in range(square // LANES):
        t = f_ref[pl.ds(n * LANES, LANES), :].T
        hi, lo = split(t)
        fcat[:width, n * LANES : (n + 1) * LANES] = hi
        fcat[width:, n * LANES : (n + 1) * LANES] = lo
    ahi, alo = split(right_ref[...])
    acat = jnp.concatenate([ahi, alo], 1)

    def outer_step(g, carry):
        at = pl.ds(pl.multiple_of(g * 2 * rows, 2 * rows), 2 * rows)
        bhi = lhi[at, :]
        o = dot(acat, jnp.concatenate([bhi, bhi], 1), 1, 1) + dot(ahi, llo[at, :], 1, 1)
        hi, lo = split(o)
        for m in range(2):
            for h2 in range(2):
                h = h2 * halves + g * 2 + m
                to = pl.ds(pl.multiple_of(h * hidden, hidden), hidden)
                for j in range(cols):
                    fro = slice((h2 * cols + j) * hidden, (h2 * cols + j + 1) * hidden)
                    ohi[to, j * rows : (j + 1) * rows] = hi[fro, m * rows : (m + 1) * rows]
                    olo[to, j * rows : (j + 1) * rows] = lo[fro, m * rows : (m + 1) * rows]
        return carry

    lax.fori_loop(0, halves // 2, outer_step, 0)

    def proj_step(g, carry):
        n = square // 4
        at = pl.ds(pl.multiple_of(g * n, n), n)
        both = dot(ohi[at, :], ccat[...], 1, 0)
        proj[at, :] = both[:, :width] + both[:, width:] + dot(olo[at, :], ccat[:, :width], 1, 0)
        return carry

    lax.fori_loop(0, 4, proj_step, 0)
    for g in range(cols // 2):
        at = slice(g * 2 * rows, (g + 1) * 2 * rows)
        both = dot(fcat[...], ohi[:, at], 1, 0)
        e = both[:width] + both[width:] + dot(fcat[:width, :], olo[:, at], 1, 0)
        edge[2 * g] = e[:, :rows].T
        edge[2 * g + 1] = e[:, rows:].T

    me = lax.axis_index("seq")
    n = len(edge_ids) // 2
    own = edge_keep.shape[1] // cols
    for k, i in enumerate(edge_ids):
        out = edge_keep if k < n else edge_send
        off = pl.multiple_of((me ^ i) * own, own)
        for j in range(cols):
            out[k % n, pl.ds(j, own, stride=cols), :] = edge[j, pl.ds(off, own), :]

    d = chunk_index(proj_bits)
    count = 1 << len(proj_bits)
    size = square // count
    for k in range(count):
        out = proj_keep if k < count // 2 else proj_send
        off = pl.multiple_of((d ^ k) * size, size)
        at = k % (count // 2)
        out[at * size : (at + 1) * size, :] = proj[pl.ds(off, size), :]


def chunk_index(bits):
    d = 0
    for axis, mask in bits:
        d = 2 * d + jnp.where((lax.axis_index(axis) & mask) != 0, 1, 0)
    return d


def sides_kernel(left_ids, cot_ids, out_ids, scale, n_left, n_cot, *refs):
    lefts, refs = refs[:n_left], refs[n_left:]
    cots, refs = refs[:n_cot], refs[n_cot:]
    right_ref, f_ref, ls_keep, ls_send, rs_ref = refs[:5]
    left, lcat, cot, cdup, clo, ghi, glo, fcat, ls = refs[5:]
    halves, rows, _ = left.shape
    cols = cot.shape[0]
    width = f_ref.shape[1]
    hidden = 2 * halves
    load_left(left_ids, lefts, left)
    load_cot(cot_ids, cots, cot)
    hi, lo = split(left[...].reshape(halves * rows, LANES))
    lcat[:, :LANES] = hi
    lcat[:, LANES:] = lo
    hi, lo = split(cot[...].reshape(cols * rows, width))
    cdup[:, :width] = hi
    cdup[:, width:] = hi
    clo[...] = lo
    hi, lo = split(f_ref[...])
    fcat[:, :width] = hi
    fcat[:, width:] = lo

    def grad_step(g, carry):
        n = 4 * hidden
        at = pl.ds(pl.multiple_of(g * n, n), n)
        f = fcat[at, :]
        for t in range(cols // 2):
            jr = slice(2 * t * rows, 2 * (t + 1) * rows)
            o = dot(f, cdup[jr, :], 1, 1) + dot(f[:, :width], clo[jr, :], 1, 1)
            hi, lo = split(o)
            for m in range(4):
                to = pl.ds(pl.multiple_of((g * 4 + m) * rows, rows), rows)
                for u in range(2):
                    j = 2 * t + u
                    fro = (slice(m * hidden, (m + 1) * hidden), slice(u * rows, (u + 1) * rows))
                    ghi[j * hidden : (j + 1) * hidden, to] = hi[fro]
                    glo[j * hidden : (j + 1) * hidden, to] = lo[fro]
        return carry

    lax.fori_loop(0, hidden // 4, grad_step, 0)

    members = LANES // 2
    rt = right_ref[: cols * hidden, :].T[:members]
    rhi, rlo = split(rt)
    rcat = jnp.concatenate([rhi, rlo], 0)

    def left_step(p, carry):
        parts = []
        for h2 in range(2):
            at = pl.ds(pl.multiple_of((h2 * halves + p) * rows, rows), rows)
            both = dot(rcat, ghi[:, at], 1, 0)
            parts.append(both[:members] + both[members:] + dot(rhi, glo[:, at], 1, 0))
        ls[p] = jnp.concatenate(parts, 0).T
        return carry

    lax.fori_loop(0, halves, left_step, 0)
    me = lax.axis_index("res")
    n = len(out_ids) // 2
    own = ls_keep.shape[2]
    for k, i in enumerate(out_ids):
        out = ls_keep if k < n else ls_send
        off = pl.multiple_of((me ^ i) * own, own)
        out[k % n] = ls[:, pl.ds(off, own), :]

    accs = []
    for h2 in range(2):
        at = slice(h2 * halves * rows, (h2 + 1) * halves * rows)
        both = dot(ghi[:, at], lcat[...], 1, 0)
        accs.append(both[:, :LANES] + both[:, LANES:] + dot(glo[:, at], lcat[:, :LANES], 1, 0))
    rs_ref[...] = (accs[0] + pltpu.roll(accs[1], LANES // 2, 1)) * scale


def back(y, inv, u):
    first = jnp.mean(u, axis=-1, keepdims=True)
    second = jnp.mean(u * y, axis=-1, keepdims=True)
    return inv * (u - first - y * second)


def upstream(a, w_ref):
    ahi, alo = split(a)
    whi, wlo = split(w_ref[...])
    lhs = jnp.concatenate([ahi, ahi, alo], 0)
    rhs = jnp.concatenate([whi, wlo, whi], 0)
    return dot(lhs, rhs, 0, 0)


def weight_grad(a, y):
    ahi, alo = split(a)
    yhi, ylo = split(y)
    n = a.shape[0]
    both = dot(jnp.concatenate([ahi, alo], 0), yhi, 1, 0)
    return both[:n] + both[n:] + dot(ahi, ylo, 1, 0)


def cols_back_kernel(count, members, rs_ref, y_ref, inv_ref, w_ref, cot_ref, out_ref, small_ref, tiles):
    hidden = w_ref.shape[0]
    low = low_half((hidden, LANES))
    total = jnp.zeros((hidden, w_ref.shape[1]), F32)
    for p in range(count // 2):
        a = rs_ref[pl.ds(2 * p * hidden, hidden), :]
        b = pltpu.roll(rs_ref[pl.ds((2 * p + 1) * hidden, hidden), :], LANES // 2, 1)
        a = jnp.where(low, a, b)
        at = pl.ds(p * LANES, LANES)
        y = y_ref[at, :]
        total = total + weight_grad(a, y)
        g = back(y, inv_ref[at, :], upstream(a, w_ref))
        for m in range(2):
            for t in range(2):
                part = g[m * members : (m + 1) * members, t * LANES : (t + 1) * LANES]
                tiles[t, pl.ds(2 * p + m, members, stride=count), :] = part
    from_tiles(tiles, out_ref)
    small_ref[:hidden, :] = total[:, :LANES]
    small_ref[hidden : 2 * hidden, :] = total[:, LANES:]
    b = jnp.sum(cot_ref[...], axis=0, keepdims=True)
    small_ref[2 * hidden :, :] = jnp.broadcast_to(b, (8, LANES))


def left_grad_kernel(count, members, keep_ref, recv_ref, y_ref, gk_ref, gr_ref, small_ref, tail_ref, a_ref, ls):
    half = ls.shape[0] // count
    hidden = 2 * half
    ls[...] = keep_ref[...] + recv_ref[...]
    low = low_half((half, LANES))
    total = jnp.zeros((hidden, y_ref.shape[1]), F32)

    def step(g, total):
        parts = []
        for t in range(2):
            v = ls[pl.ds(g * 4 + 2 * t, half, stride=count), :]
            w = ls[pl.ds(g * 4 + 2 * t + 1, half, stride=count), :]
            top = jnp.where(low, v, pltpu.roll(w, LANES // 2, 1))
            bot = jnp.where(low, pltpu.roll(v, LANES // 2, 1), w)
            parts.append(jnp.concatenate([top, bot], 0))
        a = jnp.concatenate(parts, 1)
        a_ref[g] = a
        n = 4 * members
        return total + weight_grad(a, y_ref[pl.ds(pl.multiple_of(g * n, n), n), :])

    total = lax.fori_loop(0, count // 4, step, total)
    n = gk_ref.shape[0]
    tail_ref[:n, :] = gk_ref[...] + gr_ref[...]
    tail_ref[n : n + hidden, :] = total[:, :LANES]
    tail_ref[n + hidden : n + 2 * hidden, :] = total[:, LANES:]
    tail_ref[n + 2 * hidden :, :] = small_ref[...]


def rows_back_kernel(count, members, a_ref, y_ref, inv_ref, w_ref, out_ref, tiles):
    def step(g, carry):
        u = upstream(a_ref[g], w_ref)
        n = 4 * members
        at = pl.ds(pl.multiple_of(g * n, n), n)
        r = back(y_ref[at, :], inv_ref[at, :], u)
        for m in range(4):
            for t in range(2):
                part = r[m * members : (m + 1) * members, t * LANES : (t + 1) * LANES]
                tiles[t, pl.ds(g * 4 + m, members, stride=count), :] = part
        return carry

    lax.fori_loop(0, count // 4, step, 0)
    from_tiles(tiles, out_ref)


def merge_kernel(n, a_ref, b_ref, out_ref):
    out_ref[:n, :] = a_ref[:n, :]
    out_ref[n : 2 * n, :] = b_ref[:n, :]
    out_ref[2 * n :, :] = a_ref[n:, :] + b_ref[n:, :]


def finish_kernel(bits, hidden, n, a_ref, b_ref, proj_ref, left_ref, right_ref, bias_ref):
    d = chunk_index(bits)
    count = 1 << len(bits)
    size = 2 * n // count
    for k in range(count):
        fro = a_ref if k < count // 2 else b_ref
        at = (k % (count // 2)) * size
        off = pl.multiple_of((d ^ k) * size, size)
        proj_ref[pl.ds(off, size), :] = fro[at : at + size, :]
    small = a_ref[n:, :] + b_ref[n:, :]
    for k, ref in enumerate((left_ref, right_ref)):
        ref[:, :LANES] = small[2 * k * hidden : (2 * k + 1) * hidden]
        ref[:, LANES:] = small[(2 * k + 1) * hidden : (2 * k + 2) * hidden]
    bias_ref[...] = small[4 * hidden : 4 * hidden + 1]


def body(target, source, w_source, w_target, w_final, bias, cot):
    members, cols, channels = target.shape
    own_res = source.shape[1]
    hidden = w_source.shape[1]
    square, width = w_final.shape
    own_rows = cot.shape[0]
    n_res, n_seq = lax.axis_size("res"), lax.axis_size("seq")
    rows = own_res * n_res
    scale = 1.0 / (members * n_seq)
    assert 2 * members == LANES and width == LANES and rows == LANES and channels == 2 * LANES
    half = hidden // 2
    res_bits, seq_bits = masks("res"), masks("seq")

    ws, wt = w_source.T, w_target.T
    cot_own = cot.reshape(own_rows * cols, width)
    left, row_y, row_inv = call(
        functools.partial(rows_kernel, own_res, members),
        [(half * own_res, LANES), (own_res * members, channels), (own_res * members, 1)],
        [source.reshape(members * own_res, channels), ws],
        scratch=[pltpu.VMEM((2, members * own_res, LANES), F32)],
        flops=4 * source.size * hidden, name="rows",
    )
    right, col_y, col_inv = call(
        functools.partial(cols_kernel, cols, members, scale),
        [(2 * cols * hidden, LANES), (cols * members, channels), (cols * members, 1)],
        [target.reshape(members * cols, channels), wt],
        scratch=[pltpu.VMEM((2, members * cols, LANES), F32)],
        flops=4 * target.size * hidden, name="cols",
    )

    cots, cot_ids, cur, ids = [cot_own], [0], cot_own, [0]
    for k, mask in enumerate(seq_bits):
        got = swap(cur, "seq", mask)
        cots.append(got)
        new = [i ^ mask for i in ids]
        cot_ids = cot_ids + new
        ids = ids + new
        if k + 1 < len(seq_bits):
            cur = jnp.concatenate([cur, got], 0)

    lefts, left_ids = [left.reshape(half, own_res, LANES)], [0]
    for mask in res_bits[::-1]:
        lefts = lefts + [swap(x, "res", mask) for x in lefts]
        left_ids = left_ids + [i ^ mask for i in left_ids]

    edge_ids = xor_ids(seq_bits)
    all_bits = [("res", m) for m in res_bits] + [("seq", m) for m in seq_bits]
    halvings = 0
    while halvings < len(all_bits) and (square >> (halvings + 1)) % 8 == 0:
        halvings += 1
    proj_bits, rest_bits = all_bits[:halvings], all_bits[halvings:]
    unit = cols * rows
    edge_keep, edge_send, proj_keep, proj_send = call(
        functools.partial(outer_kernel, left_ids, cot_ids, edge_ids, proj_bits, len(lefts), len(cots)),
        [(n_seq // 2, own_rows * cols, width)] * 2 + [(square // 2, width)] * 2,
        [*lefts, *cots, right, w_final],
        scratch=[
            pltpu.VMEM((half, rows, LANES), F32),
            pltpu.VMEM((half * rows, LANES), BF16),
            pltpu.VMEM((half * rows, LANES), BF16),
            pltpu.VMEM((square, unit), BF16),
            pltpu.VMEM((square, unit), BF16),
            pltpu.VMEM((cols, rows, width), F32),
            pltpu.VMEM((unit, 2 * width), BF16),
            pltpu.VMEM((2 * width, square), BF16),
            pltpu.VMEM((cols, rows, width), F32),
            pltpu.VMEM((square, width), F32),
        ],
        flops=6 * unit * square * (members + 2 * width), name="outer",
    )
    ls_ids = xor_ids(res_bits)
    ls_keep, ls_send, grad_rs = call(
        functools.partial(sides_kernel, left_ids, cot_ids, ls_ids, scale, len(lefts), len(cots)),
        [(n_res // 2, half, own_res, LANES)] * 2 + [(cols * hidden, LANES)],
        [*lefts, *cots, right, w_final],
        scratch=[
            pltpu.VMEM((half, rows, LANES), F32),
            pltpu.VMEM((half * rows, 2 * LANES), BF16),
            pltpu.VMEM((cols, rows, width), F32),
            pltpu.VMEM((unit, 2 * width), BF16),
            pltpu.VMEM((unit, width), BF16),
            pltpu.VMEM((cols * hidden, hidden * rows), BF16),
            pltpu.VMEM((cols * hidden, hidden * rows), BF16),
            pltpu.VMEM((square, 2 * width), BF16),
            pltpu.VMEM((half, rows, LANES), F32),
        ],
        flops=6 * unit * square * (2 * members + width), name="sides",
    )

    def halve(keep, send, bits):
        for k, (axis, mask) in enumerate(bits):
            got = swap(send, axis, mask)
            if k + 1 == len(bits):
                return keep, got
            n = keep.shape[0] // 2
            send = keep[n:] + got[n:]
            keep = keep[:n] + got[:n]

    proj_keep, proj_got = halve(proj_keep, proj_send, proj_bits)
    if rest_bits:
        proj_keep, proj_got = proj_keep + proj_got, jnp.zeros_like(proj_keep)
        for axis, mask in rest_bits:
            proj_keep = proj_keep + swap(proj_keep, axis, mask)
    edge_keep, edge_got = halve(edge_keep, edge_send, [("seq", m) for m in seq_bits])
    edge = (edge_keep + edge_got + bias).reshape(own_rows, cols, width)
    ls_keep, ls_got = halve(ls_keep, ls_send, [("res", m) for m in res_bits])

    grad_cols, small = call(
        functools.partial(cols_back_kernel, cols, members),
        [(members * cols, channels), (2 * hidden + 8, LANES)],
        [grad_rs, col_y, col_inv, wt, cot_own],
        scratch=[pltpu.VMEM((2, members * cols, LANES), F32)],
        flops=8 * target.size * hidden, name="cols_back",
    )
    n = proj_keep.shape[0]
    n_small = 4 * hidden + 8
    flat = half * own_res
    tail, packed = call(
        functools.partial(left_grad_kernel, own_res, members),
        [(n + n_small, LANES), (own_res // 4, hidden, 4 * members)],
        [ls_keep.reshape(flat, LANES), ls_got.reshape(flat, LANES), row_y, proj_keep, proj_got, small],
        scratch=[pltpu.VMEM((flat, LANES), F32)],
        flops=4 * source.size * hidden, name="left_grad",
    )
    (grad_rows,) = call(
        functools.partial(rows_back_kernel, own_res, members),
        [(members * own_res, channels)],
        [packed, row_y, row_inv, ws],
        scratch=[pltpu.VMEM((2, members * own_res, LANES), F32)],
        flops=8 * source.size * hidden, name="rows_back",
    )
    for axis, mask in rest_bits[::-1]:
        head, small = tail[:n], tail[n:]
        tail = jnp.concatenate([head, small + swap(small, axis, mask)], 0)
    for axis, mask in proj_bits[:0:-1]:
        (tail,) = call(
            functools.partial(merge_kernel, n), [(2 * n + n_small, LANES)], [tail, swap(tail, axis, mask)], name="merge"
        )
        n *= 2
    axis, mask = proj_bits[0]
    grad_proj, g_left, g_right, g_bias = call(
        functools.partial(finish_kernel, proj_bits, hidden, n),
        [(square, width), (hidden, channels), (hidden, channels), (1, width)],
        [tail, swap(tail, axis, mask)],
        name="finish",
    )
    return (
        edge,
        grad_cols.reshape(members, cols, channels),
        grad_rows.reshape(members, own_res, channels),
        g_left.T,
        g_right.T,
        grad_proj,
        g_bias.reshape(width),
    )


def solution(mesh):
    spec = P("seq", "res", None)
    return jax.shard_map(
        body,
        mesh=mesh,
        in_specs=(spec, spec, P(), P(), P(), P(), spec),
        out_specs=(spec, spec, spec, P(), P(), P(), P()),
        check_vma=False,
    )
```
